512 devices in a mesh: seq: 64 (over z, y), head: 8 (over x, core).
Axes of the slice: x: 4, y: 4, z: 16, core: 2. Of those that a mesh axis runs over, the one named last changes fastest.
Arguments:
- queries: bfloat16 [32768, 8, 512], P('seq', 'head'), may hold values from -8 to 8
- token_keys: bfloat16 [32768, 8, 512], P('seq', 'head'), may hold values from -8 to 8
- token_values: bfloat16 [32768, 8, 512], P('seq', 'head'), may hold values from -8 to 8
- fast_weights: bfloat16 [512, 8, 3, 512], P(None, 'head'), may hold values from -0.25 to 0.25
- learn_rate: float32 [8], P('head'), may hold values from 1 to 10
- out_gain: float32 [8, 512], P('head'), may hold values from 0.5 to 1.5
- group_lengths: int32 [2], replicated, may hold values from 1 to 24576, 32768 in all
- slot_order: int32 [32768], P('seq'), may hold values from 0 to 32767, as said below
Outputs:
- balanced_out: bfloat16 [32768, 8, 512], P('seq', 'head')
The draws below stay inside these ranges and needn't reach their ends.
Inputs may be any that keep to these rules, and one draw needn't show every extreme that they name: slot_order is a permutation of the positions; slot j, with r = j % 512, holds a position of the block [e * 512, (e + 1) * 512) with e = r // 8. `group_lengths`: the two lengths sum to 32768; each lies between 8192 and 24576.
All inputs are finite; a program needn't handle non-finite values.
Results may differ from the reference program's by a relative error of at most 0.0075.
Values may be sent and summed in bfloat16 or wider, within the bound.
A program may use at most 64 MiB of HBM per device.

```python
import math
import jax
import jax.numpy as jnp
import numpy as np
from jax import lax

HEADS = 8
HEAD_DIM = 512
FAST_HIDDEN = 512
WINDOW = 2048
TOK_DEV = 512
TOKENS = 32768


def paired_rows(key):
    array_shape = (TOKENS, HEADS, HEAD_DIM)
    query_source = jax.random.fold_in(key, 101)
    key_source = jax.random.fold_in(key, 102)
    query_rows = jax.random.truncated_normal(query_source, -6.0, 6.0, array_shape, jnp.float32)
    key_rows = jax.random.truncated_normal(key_source, -6.0, 6.0, array_shape, jnp.float32)
    return (query_rows.astype(jnp.bfloat16), key_rows.astype(jnp.bfloat16))


def draw_queries(key, part):
    return paired_rows(key)[0]


def draw_token_keys(key, part):
    return paired_rows(key)[1]


def draw_token_values(key, part):
    array_shape = (TOKENS, HEADS, HEAD_DIM)
    head_pos = jnp.arange(HEADS, dtype=jnp.float32) / max(HEADS - 1, 1)
    scales = 0.6 * 3.0 ** head_pos
    base = jax.random.truncated_normal(key, -4.0, 4.0, array_shape, jnp.float32)
    return (base * scales[None, :, None]).astype(jnp.bfloat16)


def draw_slot_order(key, part):
    source_count = TOKENS // TOK_DEV
    seg_rows = TOK_DEV // source_count
    block_keys = jax.random.split(key, source_count)
    shuffled = jax.vmap(lambda block_key: jax.random.permutation(block_key, TOK_DEV))(block_keys)
    placed = shuffled.astype(jnp.int32) + (jnp.arange(source_count, dtype=jnp.int32) * TOK_DEV)[:, None]
    placed = placed.reshape(source_count, source_count, seg_rows)
    return jnp.transpose(placed, (1, 0, 2)).reshape(TOKENS).astype(jnp.int32)


def levels(stream_key, extent, cuts, smallest, high):
    def one(axis_at, parts):
        draws = jax.random.uniform(jax.random.fold_in(jax.random.fold_in(stream_key, 6), axis_at), (parts,), jnp.float32, smallest / len(cuts), high / len(cuts))
        return jnp.repeat(jnp.exp(draws), extent[axis_at] // parts).reshape((-1,) + (1,) * (len(extent) - axis_at - 1))

    factor_of = one(*cuts[0])
    for cut in cuts[1:]:
        factor_of = factor_of * one(*cut)
    return factor_of


def split_up(count, total, most, skew):
    loads = [(1 << 20) // math.isqrt(grade ** skew) + 1 for grade in range(2, count + 1)]
    surplus, given = total - most - (count - 1), [1] * (count - 1)
    while surplus > 0:
        free = [i for i in range(count - 1) if given[i] < most]
        mass, remaining = sum([loads[i] for i in free]), surplus
        for i in free:
            extra = min(most - given[i], max(1, remaining * loads[i] // mass), surplus)
            given[i] = given[i] + extra
            surplus = surplus - extra
    return np.array([most] + given)


def uneven_parts(key, count, total, limit, slope):
    if count == 2:
        one = jax.random.randint(key, (), max(1, total - limit), min(limit, total - 1) + 1)
        return jnp.stack([one, total - one])
    tallies = jnp.asarray(split_up(count, total, limit, slope), jnp.int32)
    couples = (count - 1) // 2
    donor, taker = tallies[1:1 + 2 * couples:2], tallies[2:2 + 2 * couples:2]
    room = jnp.minimum(donor - 1, limit - taker)
    shifted = jax.random.randint(jax.random.fold_in(key, 1), (couples,), 0, 1 << 20) % (room + 1)
    tallies = tallies.at[1:1 + 2 * couples:2].set(donor - shifted).at[2:2 + 2 * couples:2].set(taker + shifted)
    return tallies[jax.random.permutation(jax.random.fold_in(key, 2), count)]


def noise(own_key, extent, deviation, most, cuts=(), kind=jnp.bfloat16):
    drawn = jax.random.normal(own_key, extent, jnp.float32) * deviation
    if len(cuts) > 0:
        drawn = levels(own_key, extent, cuts, -0.22, 0.18) * drawn
    return jnp.clip(drawn, min=-most, max=most).astype(kind)


def setup_inputs(seed: int = 0) -> dict:
    keys = jax.random.split(jax.random.key(seed), 9)
    queries = draw_queries(jax.random.fold_in(keys[8], 71), 0)
    token_keys = draw_token_keys(jax.random.fold_in(keys[8], 71), 0)
    token_values = draw_token_values(jax.random.fold_in(keys[8], 71), 0)
    fast_weights = noise(keys[3], (FAST_HIDDEN, HEADS, 3, HEAD_DIM), HEAD_DIM ** -0.5, 0.25, ((1, 8),))
    learn_rate = jnp.clip(jnp.exp(math.log(10.0) - 2.3025851 * jax.random.uniform(keys[4], (HEADS,), jnp.float32) ** levels(keys[4], (HEADS,), ((0, 8),), -0.2, 0.2)), 1.0, 10.0)
    out_gain = jnp.clip(1.0 + 0.1 * jax.random.normal(keys[5], (HEADS, HEAD_DIM), jnp.float32), 0.5, 1.5)
    group_lengths = uneven_parts(keys[6], 2, TOKENS, TOKENS * 3 // 4, 0).astype(jnp.int32)
    slot_order = draw_slot_order(jax.random.fold_in(keys[8], 71), 0)
    return {"queries": queries, "token_keys": token_keys, "token_values": token_values, "fast_weights": fast_weights, "learn_rate": learn_rate, "out_gain": out_gain, "group_lengths": group_lengths, "slot_order": slot_order}


eps = 1e-06

def head_attention(query_head, key_head, value_head):
    block_rows = 512
    padded_keys = jnp.concatenate([jnp.zeros((WINDOW, HEAD_DIM), key_head.dtype), key_head], axis=0)
    padded_values = jnp.concatenate([jnp.zeros((WINDOW, HEAD_DIM), value_head.dtype), value_head], axis=0)
    score_scale = 1.0 / math.sqrt(HEAD_DIM)

    def attend(block_index):
        first_row = block_index * block_rows
        query_rows = lax.dynamic_slice_in_dim(query_head, first_row, block_rows, 0)
        key_rows = lax.dynamic_slice_in_dim(padded_keys, first_row, WINDOW + block_rows, 0)
        value_rows = lax.dynamic_slice_in_dim(padded_values, first_row, WINDOW + block_rows, 0)
        scores = jnp.dot(query_rows, key_rows.T, preferred_element_type=jnp.float32) * score_scale
        query_pos = first_row + jnp.arange(block_rows, dtype=jnp.int32)[:, None]
        key_pos = first_row - WINDOW + jnp.arange(WINDOW + block_rows, dtype=jnp.int32)[None, :]
        allowed = (key_pos <= query_pos) & (key_pos > query_pos - WINDOW) & (key_pos >= 0)
        scores = jnp.where(allowed, scores, -jnp.inf)
        row_max = lax.optimization_barrier(jnp.max(scores, axis=-1, keepdims=True))
        expo = jnp.exp(scores - row_max)
        prob_rows = (expo / lax.optimization_barrier(jnp.sum(expo, axis=-1, keepdims=True))).astype(jnp.bfloat16)
        return jnp.dot(prob_rows, value_rows, preferred_element_type=jnp.float32).astype(jnp.bfloat16)
    blocks = lax.map(attend, jnp.arange(TOKENS // block_rows, dtype=jnp.int32))
    return blocks.reshape(TOKENS, HEAD_DIM)

def swiglu_rows(inputs, weights):
    gate_pre = jnp.dot(inputs, weights[:, 0, :].T, preferred_element_type=jnp.float32)
    up_pre = jnp.dot(inputs, weights[:, 1, :].T, preferred_element_type=jnp.float32)
    hidden_act = (jax.nn.silu(gate_pre) * up_pre).astype(jnp.bfloat16)
    return jnp.dot(hidden_act, weights[:, 2, :], preferred_element_type=jnp.float32).astype(jnp.bfloat16)

def head_fast(query_head, key_head, value_head, weight_head, rate_value, first_len):
    member = jnp.arange(TOKENS, dtype=jnp.int32) < first_len
    group_count = first_len.astype(jnp.float32)
    gate_pre = jnp.dot(key_head, weight_head[:, 0, :].T, preferred_element_type=jnp.float32)
    up_pre = jnp.dot(key_head, weight_head[:, 1, :].T, preferred_element_type=jnp.float32)
    activation = (jax.nn.silu(gate_pre) * up_pre).astype(jnp.bfloat16)
    masked_values = jnp.where(member[:, None], value_head, jnp.zeros_like(value_head))
    back_act = jnp.dot(masked_values, weight_head[:, 2, :].T, preferred_element_type=jnp.float32)
    sig_gate = jax.nn.sigmoid(gate_pre)
    grad_up = (back_act * gate_pre * sig_gate).astype(jnp.bfloat16)
    grad_gate = (back_act * up_pre * sig_gate * (1.0 + gate_pre * (1.0 - sig_gate))).astype(jnp.bfloat16)
    term_gate = jnp.dot(grad_gate.T, key_head, preferred_element_type=jnp.float32)
    term_up = jnp.dot(grad_up.T, key_head, preferred_element_type=jnp.float32)
    term_down = jnp.dot(activation.T, masked_values, preferred_element_type=jnp.float32)
    summed = jnp.stack([term_gate, term_up, term_down], axis=1)
    previous = weight_head.astype(jnp.float32)
    updated = previous + rate_value / group_count * summed
    old_norm = jnp.sqrt(lax.optimization_barrier(jnp.sum(previous * previous, axis=-1, keepdims=True)) + eps)
    new_norm = jnp.sqrt(lax.optimization_barrier(jnp.sum(updated * updated, axis=-1, keepdims=True)) + eps)
    new_weights = (updated * (old_norm / new_norm)).astype(jnp.bfloat16)
    first_out = swiglu_rows(query_head, weight_head)
    second_out = swiglu_rows(query_head, new_weights)
    return jnp.where(member[:, None], first_out, second_out)

def reference(queries, token_keys, token_values, fast_weights, learn_rate, out_gain, group_lengths, slot_order):
    first_len = group_lengths[0]
    head_queries = jnp.swapaxes(queries, 0, 1)
    head_keys = jnp.swapaxes(token_keys, 0, 1)
    head_values = jnp.swapaxes(token_values, 0, 1)
    attention = lax.map(lambda packed: head_attention(packed[0], packed[1], packed[2]), (head_queries, head_keys, head_values))
    head_weights = jnp.transpose(fast_weights, (1, 0, 2, 3))
    fast_out = lax.map(lambda packed: head_fast(packed[0], packed[1], packed[2], packed[3], packed[4], first_len), (head_queries, head_keys, head_values, head_weights, learn_rate))
    summed_rows = jnp.swapaxes(attention.astype(jnp.float32) + fast_out.astype(jnp.float32), 0, 1)
    power = lax.optimization_barrier(jnp.mean(summed_rows * summed_rows, axis=(1, 2)))
    normed = summed_rows * lax.rsqrt(power + eps)[:, None, None] * out_gain[None, :, :]
    return jnp.take(normed, slot_order.astype(jnp.int32), axis=0).astype(jnp.bfloat16)
```

```python
import functools
import math

import jax
import jax.numpy as jnp
from jax import lax
from jax.experimental import pallas as pl
from jax.experimental.pallas import tpu as pltpu
from jax.sharding import PartitionSpec as P

WINDOW = 2048
CHUNKS = 8
eps = 1e-06
MESH = pl.DeviceIdType.MESH
f32 = jnp.float32
bf16 = jnp.bfloat16


def dot_t(a, b):
    return lax.dot_general(a, b, (((1,), (1,)), ((), ())), preferred_element_type=f32)


def dot_n(a, b):
    return jnp.dot(a, b, preferred_element_type=f32)


def layer_kernel(
    Y, Z, H, UP, DOWN, WIN,
    q_hbm, k_hbm, v_hbm, w_hbm, lr_ref, gain_ref, len_ref, slot_ref,
    out_ref,
    q, kv, w, relay, grad, rs_send_p, rs_send_m, rs_recv_p, rs_recv_m,
    total, y_send, y_recv, new_w, acc, row_m, row_l, first_out, rows,
    power, wanted, asked, send_rows,
    load_sem, win_send, win_recv, relay_send, relay_recv, fwd_send, mid_recv,
    rsp_send, rsp_recv, rsm_send, rsm_recv, ys_send, ys_recv,
    agp_send, agp_recv, agm_send, agm_recv,
    pow_send, pow_recv, idx_send, idx_recv, a2a_send, a2a_recv, own_sem,
):
    T, D = q.shape
    F = w.shape[1]
    FR = F // Z
    N = Y * Z
    SEG = T // N
    CR = T // CHUNKS
    s = lax.axis_index("seq")
    h = lax.axis_index("head")
    z = s // Y
    y = s % Y

    def seq_at(zz, yy):
        return lax.rem(zz + Z, Z) * Y + lax.rem(yy + Y, Y)

    up = seq_at(z + 1, y)
    down = seq_at(z - 1, y)

    def remote(src, dst, ssem, rsem, seq):
        return pltpu.make_async_remote_copy(
            src_ref=src, dst_ref=dst, send_sem=ssem, recv_sem=rsem,
            device_id={"seq": seq}, device_id_type=MESH,
        )

    loads = [
        pltpu.make_async_copy(k_hbm, kv.at[0, 0], load_sem.at[0]),
        pltpu.make_async_copy(v_hbm, kv.at[0, 1], load_sem.at[1]),
        pltpu.make_async_copy(w_hbm, w, load_sem.at[2]),
        pltpu.make_async_copy(q_hbm, q, load_sem.at[3]),
    ]
    for copy in loads:
        copy.start()

    barrier = pltpu.get_barrier_semaphore()
    near = [up, down] + [seq_at(z, y + k) for k in range(1, Y)]
    for partner in near:
        pl.semaphore_signal(barrier, inc=1, device_id={"seq": partner}, device_id_type=MESH)
    for k in range(1, H):
        pl.semaphore_signal(
            barrier, inc=1, device_id={"head": lax.rem(h + k, H)}, device_id_type=MESH
        )
    for g in range(128 // SEG):
        line = slot_ref[...] if g == 0 else pltpu.roll(slot_ref[...], 128 - SEG * g, 1)
        for i in range(T // 128):
            e = i * (128 // SEG) + g
            wanted[e] = line[i : i + 1, :] - e * T
    pl.semaphore_wait(barrier, len(near) + H - 1)
    loads[0].wait()
    loads[1].wait()

    def rows_of(i):
        return pl.ds(i * CR, CR)

    def zhop(i):
        return remote(
            kv.at[0, :, rows_of(i)], kv.at[Y, :, rows_of(i)],
            win_send.at[Y, i], win_recv.at[Y, i], up,
        )

    def spread(src, k, i):
        if k != 2:
            return [
                remote(
                    kv.at[src, :, rows_of(i)], kv.at[k, :, rows_of(i)],
                    win_send.at[k, i], win_recv.at[k, i], seq_at(z, y + k),
                )
            ]
        return [over(src, j, i) for j in range(2)]

    def over(src, j, i):
        return remote(
            kv.at[src, j, rows_of(i)], relay.at[j, rows_of(i)],
            relay_send.at[j, i], relay_recv.at[j, i], seq_at(z, y + (1 if j == 0 else -1)),
        )

    def forward(j, i):
        return remote(
            relay.at[j, rows_of(i)], kv.at[2, j, rows_of(i)],
            fwd_send.at[j, i], mid_recv.at[j, i], seq_at(z, y + (1 if j == 0 else -1)),
        )

    order = [1, 3, 2]
    zhop(0).start()
    for k in order:
        @pl.when(y + k < Y)
        def _():
            for i in range(CHUNKS):
                for copy in spread(0, k, i):
                    copy.start()

    def window_step(i):
        zhop(i).wait_recv()
        for k in order:
            @pl.when(y + k >= Y)
            def _():
                for copy in spread(Y, k, i):
                    copy.start()
        for j in range(2):
            over(0, j, i).wait_recv()
            forward(j, i).start()

    first_len = len_ref[0]
    lane_member = (s * T + lax.broadcasted_iota(jnp.int32, (1, T), 1)) < first_len
    loads[2].wait()
    keys = kv[0, 0]
    values = kv[0, 1]
    gate_pre = dot_t(w[0], keys)
    up_pre = dot_t(w[1], keys)
    sig_gate = jax.nn.sigmoid(gate_pre)
    gated = gate_pre * sig_gate
    activation = jnp.where(lane_member, gated * up_pre, 0.0).astype(bf16)
    back = jnp.where(lane_member, dot_t(w[2], values), 0.0)
    grad_up = (back * gated).astype(bf16)
    grad_gate = (back * up_pre * sig_gate * (1.0 + gate_pre * (1.0 - sig_gate))).astype(bf16)

    def chunk_of(zz):
        return lax.rem(zz + 2 * Z, Z)

    def piece(c, zz):
        return grad[c, pl.ds(pl.multiple_of(chunk_of(zz) * FR, FR), FR), :]

    def rs_up(t, c):
        return remote(
            rs_send_p.at[t, c], rs_recv_p.at[t, c], rsp_send.at[t, c], rsp_recv.at[t, c], up
        )

    def rs_down(t, c):
        return remote(
            rs_send_m.at[t, c], rs_recv_m.at[t, c], rsm_send.at[t, c], rsm_recv.at[t, c], down
        )

    def rs_step(t, c):
        if t < DOWN:
            value = piece(c, z - DOWN + t)
            if t > 0:
                rs_down(t - 1, c).wait_recv()
                value = value + rs_recv_m[t - 1, c].astype(f32)
            rs_send_m[t, c] = value.astype(bf16)
            rs_down(t, c).start()
        if t < UP:
            value = piece(c, z + UP - t)
            if t > 0:
                rs_up(t - 1, c).wait_recv()
                value = value + rs_recv_p[t - 1, c].astype(f32)
            rs_send_p[t, c] = value.astype(bf16)
            rs_up(t, c).start()

    grad[2] = dot_n(activation, values)
    rs_step(0, 2)
    grad[1] = dot_n(grad_up, keys)
    rs_step(0, 1)
    grad[0] = dot_n(grad_gate, keys)
    rs_step(0, 0)
    zhop(1).start()
    loads[3].wait()

    scale = 1.0 / math.sqrt(D)
    HALF = T // 2

    def attend(d, half):
        span = pl.ds(half * HALF, HALF)
        scores = dot_t(q[span, :], kv[d, 0]) * scale
        r = half * HALF + lax.broadcasted_iota(jnp.int32, (HALF, T), 0)
        col = lax.broadcasted_iota(jnp.int32, (HALF, T), 1)
        ahead = r - col + d * T
        allowed = (ahead >= 0) & (ahead < WIN) & (s * T - d * T + col >= 0)
        scores = jnp.where(allowed, scores, -jnp.inf)
        peak = jnp.max(scores, axis=1, keepdims=True)
        if d == 0:
            expo = jnp.exp(scores - peak)
            row_l[span, :] = jnp.broadcast_to(jnp.sum(expo, axis=1, keepdims=True), (HALF, 128))
            acc[span, :] = dot_n(expo.astype(bf16), kv[d, 1])
        else:
            before = row_m[span, :][:, 0:1]
            peak = jnp.maximum(before, peak)
            decay = jnp.exp(before - peak)
            expo = jnp.exp(scores - peak)
            row_l[span, :] = row_l[span, :] * decay + jnp.sum(expo, axis=1, keepdims=True)
            acc[span, :] = acc[span, :] * decay + dot_n(expo.astype(bf16), kv[d, 1])
        row_m[span, :] = jnp.broadcast_to(peak, (HALF, 128))

    def swiglu(inputs, gate_w, up_w, down_w):
        gate = dot_t(inputs, gate_w)
        hidden = (gate * jax.nn.sigmoid(gate) * dot_t(inputs, up_w)).astype(bf16)
        return dot_n(hidden, down_w).astype(bf16)

    def early_fast(half):
        span = pl.ds(half * HALF, HALF)
        first_out[span, :] = swiglu(q[span, :], w[0], w[1], w[2])

    fillers = [
        functools.partial(attend, 0, 0), functools.partial(attend, 0, 1),
        functools.partial(early_fast, 0), functools.partial(early_fast, 1),
    ]
    steps = max(UP, DOWN)
    hop, seen = 2, 0
    for t in range(1, steps):
        for c in (2, 1, 0):
            rs_step(t, c)
        if hop < CHUNKS:
            zhop(hop).start()
            hop += 1
        if seen < CHUNKS:
            window_step(seen)
            seen += 1
        if fillers:
            fillers.pop(0)()

    def y_copy(k, c):
        return remote(
            y_send.at[c], y_recv.at[k - 1, c], ys_send.at[k - 1, c], ys_recv.at[k - 1, c],
            seq_at(z, y + k),
        )

    for c in (2, 1, 0):
        value = piece(c, z)
        if DOWN > 0:
            rs_down(DOWN - 1, c).wait_recv()
            value = value + rs_recv_m[DOWN - 1, c].astype(f32)
        rs_up(UP - 1, c).wait_recv()
        value = value + rs_recv_p[UP - 1, c].astype(f32)
        total[c] = value
        y_send[c] = value.astype(bf16)
        for k in range(1, Y):
            y_copy(k, c).start()
    while hop < CHUNKS:
        zhop(hop).start()
        hop += 1
    while fillers:
        fillers.pop(0)()

    def idx_body(k, carry):
        target = lax.rem(s + k, N)
        remote(wanted.at[target], asked.at[s], idx_send, idx_recv, target).start()
        return carry

    group_count = jnp.full((1, D), first_len, jnp.int32).astype(f32)
    rate = lr_ref[0] / group_count
    for c in (2, 1, 0):
        value = total[c]
        for k in range(1, Y):
            y_copy(k, c).wait_recv()
            value = value + y_recv[k - 1, c].astype(f32)
        previous = w[c, pl.ds(pl.multiple_of(z * FR, FR), FR), :].astype(f32)
        updated = previous + rate * value
        old_norm = jnp.sqrt(jnp.sum(previous * previous, axis=1, keepdims=True) + eps)
        new_norm = jnp.sqrt(jnp.sum(updated * updated, axis=1, keepdims=True) + eps)
        new_w[z, c] = (updated * (old_norm / new_norm)).astype(bf16)

    def ag_up(t, c):
        at = chunk_of(z - t)
        return remote(new_w.at[at, c], new_w.at[at, c], agp_send.at[t, c], agp_recv.at[t, c], up)

    def ag_down(t, c):
        at = chunk_of(z + t)
        return remote(new_w.at[at, c], new_w.at[at, c], agm_send.at[t, c], agm_recv.at[t, c], down)

    def ag_wait_up(t, c):
        at = chunk_of(z - 1 - t)
        remote(
            new_w.at[at, c], new_w.at[at, c], agp_send.at[t, c], agp_recv.at[t, c], up
        ).wait_recv()

    def ag_wait_down(t, c):
        at = chunk_of(z + 1 + t)
        remote(
            new_w.at[at, c], new_w.at[at, c], agm_send.at[t, c], agm_recv.at[t, c], down
        ).wait_recv()

    def block_ready(d):
        for i in range(CHUNKS):
            if d == 2:
                for j in range(2):
                    forward(j, i).wait_recv()
            elif d != Y:
                spread(0, d, i)[0].wait_recv()

    def block(d, half):
        if half == 0:
            block_ready(d)
        attend(d, half)

    fillers = [functools.partial(block, d, half) for d in (Y, 1, 3, 2) for half in range(2)]
    for t in range(steps):
        for c in (2, 1, 0):
            if t < DOWN:
                if t > 0:
                    ag_wait_down(t - 1, c)
                ag_down(t, c).start()
            if t < UP:
                if t > 0:
                    ag_wait_up(t - 1, c)
                ag_up(t, c).start()
        if t == 0:
            lax.fori_loop(1, N, idx_body, 0)
            asked[s] = wanted[s]
        if seen < CHUNKS:
            window_step(seen)
            seen += 1
        elif fillers and t >= 2:
            fillers.pop(0)()
    while seen < CHUNKS:
        window_step(seen)
        seen += 1
    while fillers:
        fillers.pop(0)()
    pltpu.make_async_copy(asked.at[pl.ds(0, N - 1)], asked.at[pl.ds(0, N - 1)], idx_recv).wait()
    attention = (acc[...] / row_l[...][:, 0:1]).astype(bf16)
    for c in (2, 1, 0):
        if DOWN > 0:
            ag_wait_down(DOWN - 1, c)
        ag_wait_up(UP - 1, c)

    second = swiglu(
        q[...], new_w[:, 0].reshape(F, D), new_w[:, 1].reshape(F, D), new_w[:, 2].reshape(F, D)
    )
    member = (s * T + lax.broadcasted_iota(jnp.int32, (T, D), 0)) < first_len
    fast = jnp.where(member, first_out[...].astype(f32), second.astype(f32))
    summed = attention.astype(f32) + fast
    rows[...] = summed
    square = summed * summed
    coarse = square.astype(bf16)
    fine = (square - coarse.astype(f32)).astype(bf16)
    ones = jnp.ones((8, D), bf16)
    power[h] = (dot_t(ones, coarse) + dot_t(ones, fine))[0:1, :]

    def pow_copy(k):
        return pltpu.make_async_remote_copy(
            src_ref=power.at[h], dst_ref=power.at[h],
            send_sem=pow_send.at[k - 1], recv_sem=pow_recv.at[k - 1],
            device_id={"head": lax.rem(h + k, H)}, device_id_type=MESH,
        )

    for k in range(1, H):
        pow_copy(k).start()
    lines = jnp.broadcast_to(asked[...].astype(f32), (N, SEG, 128)).reshape(T, 128)
    lane = lax.broadcasted_iota(jnp.int32, (T, 128), 1)
    spot = lax.rem(lax.broadcasted_iota(jnp.int32, (T, 128), 0), SEG)
    picked = jnp.sum(jnp.where(lane == spot, lines, 0.0), axis=1, keepdims=True)
    column = lax.broadcasted_iota(jnp.int32, (T, T), 1).astype(f32)
    choose = jnp.where(column == picked, 1.0, 0.0).astype(bf16)
    for k in range(1, H):
        pow_copy(k).wait_recv()
    strength = power[0]
    for k in range(1, H):
        strength = strength + power[k]
    row_scale = lax.rsqrt(strength / (H * D) + eps)
    spread_scale = jnp.broadcast_to(row_scale, (128, T)).T
    wide_scale = jnp.concatenate([spread_scale] * (D // 128), axis=1)
    normed = (rows[...] * wide_scale * gain_ref[...]).astype(bf16)
    send_rows[...] = dot_n(choose, normed).reshape(N, SEG, D).astype(bf16)

    def a2a_body(k, carry):
        target = lax.rem(s + k, N)
        remote(send_rows.at[target], out_ref.at[s], a2a_send, a2a_recv, target).start()
        return carry

    lax.fori_loop(1, N, a2a_body, 0)
    own = pltpu.make_async_copy(send_rows.at[s], out_ref.at[s], own_sem)
    own.start()

    for i in range(CHUNKS):
        zhop(i).wait_send()
        for k in order:
            for copy in spread(0, k, i):
                copy.wait_send()
        for j in range(2):
            forward(j, i).wait_send()
    for c in range(3):
        for t in range(UP):
            rs_up(t, c).wait_send()
            ag_up(t, c).wait_send()
        for t in range(DOWN):
            rs_down(t, c).wait_send()
            ag_down(t, c).wait_send()
        for k in range(1, Y):
            y_copy(k, c).wait_send()
    for k in range(1, H):
        pow_copy(k).wait_send()
    pltpu.make_async_copy(wanted.at[pl.ds(0, N - 1)], wanted.at[pl.ds(0, N - 1)], idx_send).wait()
    own.wait()
    pltpu.make_async_copy(
        send_rows.at[pl.ds(0, N - 1)], send_rows.at[pl.ds(0, N - 1)], a2a_send
    ).wait()
    pltpu.make_async_copy(
        out_ref.at[pl.ds(0, N - 1)], out_ref.at[pl.ds(0, N - 1)], a2a_recv
    ).wait()


def solution(mesh, window=WINDOW):
    N = mesh.shape["seq"]
    H = mesh.shape["head"]

    def per_device(q, k, v, weights, learn_rate, out_gain, group_lengths, slot_order):
        T, _, D = q.shape
        F = weights.shape[0]
        Y = window // T
        Z = N // Y
        UP = Z // 2
        DOWN = Z - 1 - UP
        FR = F // Z
        SEG = T // N
        dma = pltpu.SemaphoreType.DMA
        VMEM = pltpu.VMEM
        any_spec = pl.BlockSpec(memory_space=pl.ANY)
        vmem_spec = pl.BlockSpec(memory_space=pltpu.VMEM)
        smem_spec = pl.BlockSpec(memory_space=pltpu.SMEM)
        out = pl.pallas_call(
            functools.partial(layer_kernel, Y, Z, H, UP, DOWN, window),
            out_shape=jax.ShapeDtypeStruct((N, SEG, D), bf16),
            in_specs=[any_spec] * 4 + [smem_spec, vmem_spec, smem_spec, vmem_spec],
            out_specs=any_spec,
            scratch_shapes=[
                VMEM((T, D), bf16),
                VMEM((Y + 1, 2, T, D), bf16),
                VMEM((3, F, D), bf16),
                VMEM((2, T, D), bf16),
                VMEM((3, F, D), f32),
                VMEM((UP, 3, FR, D), bf16),
                VMEM((max(DOWN, 1), 3, FR, D), bf16),
                VMEM((UP, 3, FR, D), bf16),
                VMEM((max(DOWN, 1), 3, FR, D), bf16),
                VMEM((3, FR, D), f32),
                VMEM((3, FR, D), bf16),
                VMEM((Y - 1, 3, FR, D), bf16),
                VMEM((Z, 3, FR, D), bf16),
                VMEM((T, D), f32),
                VMEM((T, 128), f32),
                VMEM((T, 128), f32),
                VMEM((T, D), bf16),
                VMEM((T, D), f32),
                VMEM((H, 1, T), f32),
                VMEM((N, 1, 128), jnp.int32),
                VMEM((N, 1, 128), jnp.int32),
                VMEM((N, SEG, D), bf16),
                dma((4,)),
                dma((Y + 1, CHUNKS)),
                dma((Y + 1, CHUNKS)),
                dma((2, CHUNKS)),
                dma((2, CHUNKS)),
                dma((2, CHUNKS)),
                dma((2, CHUNKS)),
                dma((UP, 3)),
                dma((UP, 3)),
                dma((max(DOWN, 1), 3)),
                dma((max(DOWN, 1), 3)),
                dma((Y - 1, 3)),
                dma((Y - 1, 3)),
                dma((UP, 3)),
                dma((UP, 3)),
                dma((max(DOWN, 1), 3)),
                dma((max(DOWN, 1), 3)),
                dma((max(H - 1, 1),)),
                dma((max(H - 1, 1),)),
                dma,
                dma,
                dma,
                dma,
                dma,
            ],
            compiler_params=pltpu.CompilerParams(
                collective_id=0, has_side_effects=True, vmem_limit_bytes=60 * 1024 * 1024
            ),
            name="ttt_layer",
        )(
            q.reshape(T, D), k.reshape(T, D), v.reshape(T, D),
            jnp.transpose(weights.reshape(F, 3, D), (1, 0, 2)),
            learn_rate, out_gain, group_lengths, slot_order.reshape(T // 128, 128),
        )
        return out.reshape(T, 1, D)

    return jax.shard_map(
        per_device,
        mesh=mesh,
        in_specs=(
            P("seq", "head", None),
            P("seq", "head", None),
            P("seq", "head", None),
            P(None, "head", None, None),
            P("head"),
            P("head", None),
            P(),
            P("seq"),
        ),
        out_specs=P("seq", "head", None),
        check_vma=False,
    )
```

```python
import functools
import math

import jax
import jax.numpy as jnp
from jax import lax
from jax.experimental import pallas as pl
from jax.experimental.pallas import tpu as pltpu
from jax.sharding import PartitionSpec as P

WINDOW = 2048
CHUNKS = 16
UP_HOPS = 6
eps = 1e-06
MESH = pl.DeviceIdType.MESH
f32 = jnp.float32
bf16 = jnp.bfloat16


def dot_t(a, b):
    return lax.dot_general(a, b, (((1,), (1,)), ((), ())), preferred_element_type=f32)


def dot_n(a, b):
    return jnp.dot(a, b, preferred_element_type=f32)


def layer_kernel(
    Y, Z, H, UP, DOWN, WIN,
    q_hbm, k_hbm, v_hbm, w_hbm, lr_ref, gain_ref, len_ref, slot_ref,
    out_ref,
    q, kv, w, relay, grad, rs_send_p, rs_send_m, rs_recv_p, rs_recv_m,
    total, y_send, y_recv, new_w, acc, row_m, row_l, first_out, rows,
    power, wanted, asked, choose, send_rows,
    load_sem, win_send, win_recv, relay_send, relay_recv, fwd_send, mid_recv,
    rsp_send, rsp_recv, rsm_send, rsm_recv, ys_send, ys_recv,
    agp_send, agp_recv, agm_send, agm_recv,
    pow_send, pow_recv, idx_send, idx_recv, a2a_send, a2a_recv, own_sem,
):
    T, D = q.shape
    F = w.shape[1]
    FR = F // Z
    N = Y * Z
    SEG = T // N
    CR = T // CHUNKS
    s = lax.axis_index("seq")
    h = lax.axis_index("head")
    z = s // Y
    y = s % Y

    def seq_at(zz, yy):
        return lax.rem(zz + Z, Z) * Y + lax.rem(yy + Y, Y)

    up = seq_at(z + 1, y)
    down = seq_at(z - 1, y)

    def remote(src, dst, ssem, rsem, seq):
        return pltpu.make_async_remote_copy(
            src_ref=src, dst_ref=dst, send_sem=ssem, recv_sem=rsem,
            device_id={"seq": seq}, device_id_type=MESH,
        )

    loads = [
        pltpu.make_async_copy(k_hbm, kv.at[0, 0], load_sem.at[0]),
        pltpu.make_async_copy(v_hbm, kv.at[0, 1], load_sem.at[1]),
        pltpu.make_async_copy(w_hbm, w, load_sem.at[2]),
        pltpu.make_async_copy(q_hbm, q, load_sem.at[3]),
    ]
    for copy in loads:
        copy.start()

    barrier = pltpu.get_barrier_semaphore()
    near = [up, down] + [seq_at(z, y + k) for k in range(1, Y)]
    for partner in near:
        pl.semaphore_signal(barrier, inc=1, device_id={"seq": partner}, device_id_type=MESH)
    for k in range(1, H):
        pl.semaphore_signal(
            barrier, inc=1, device_id={"head": lax.rem(h + k, H)}, device_id_type=MESH
        )
    for g in range(128 // SEG):
        line = slot_ref[...] if g == 0 else pltpu.roll(slot_ref[...], 128 - SEG * g, 1)
        for i in range(T // 128):
            e = i * (128 // SEG) + g
            wanted[e] = line[i : i + 1, :] - e * T
    pl.semaphore_wait(barrier, len(near) + H - 1)
    loads[0].wait()
    loads[1].wait()

    def rows_of(i):
        return pl.ds(i * CR, CR)

    def zhop(i):
        return remote(
            kv.at[0, :, rows_of(i)], kv.at[Y, :, rows_of(i)],
            win_send.at[Y, i], win_recv.at[Y, i], up,
        )

    def spread(k, i):
        src = jnp.where(y + k < Y, 0, Y)
        return remote(
            kv.at[src, :, rows_of(i)], kv.at[k, :, rows_of(i)],
            win_send.at[k, i], win_recv.at[k, i], seq_at(z, y + k),
        )

    def over(j, i):
        src = jnp.where(y + 2 < Y, 0, Y)
        return remote(
            kv.at[src, j, rows_of(i)], relay.at[j, rows_of(i)],
            relay_send.at[j, i], relay_recv.at[j, i], seq_at(z, y + (1 if j == 0 else -1)),
        )

    def forward(j, i):
        return remote(
            relay.at[j, rows_of(i)], kv.at[2, j, rows_of(i)],
            fwd_send.at[j, i], mid_recv.at[j, i], seq_at(z, y + (1 if j == 0 else -1)),
        )

    AHEAD = 3
    for i in range(AHEAD):
        zhop(i).start()

    def window_step(i):
        if i < CHUNKS:
            if i + AHEAD < CHUNKS:
                zhop(i + AHEAD).start()
            zhop(i).wait_recv()
            for j in range(2):
                over(j, i).start()
            spread(1, i).start()
            spread(3, i).start()
        if 1 <= i <= CHUNKS:
            for j in range(2):
                over(j, i - 1).wait_recv()
                forward(j, i - 1).start()

    first_len = len_ref[0]
    lane_member = (s * T + lax.broadcasted_iota(jnp.int32, (1, T), 1)) < first_len
    loads[2].wait()
    keys = kv[0, 0]
    values = kv[0, 1]
    gate_pre = dot_t(w[0], keys)
    up_pre = dot_t(w[1], keys)
    sig_gate = jax.nn.sigmoid(gate_pre)
    gated = gate_pre * sig_gate
    activation = jnp.where(lane_member, gated * up_pre, 0.0).astype(bf16)
    back = jnp.where(lane_member, dot_t(w[2], values), 0.0)
    grad_up = (back * gated).astype(bf16)
    grad_gate = (back * up_pre * sig_gate * (1.0 + gate_pre * (1.0 - sig_gate))).astype(bf16)

    def chunk_of(zz):
        return lax.rem(zz + 2 * Z, Z)

    def piece(c, zz):
        return grad[c, pl.ds(pl.multiple_of(chunk_of(zz) * FR, FR), FR), :]

    def rs_up(t, c):
        return remote(
            rs_send_p.at[t, c], rs_recv_p.at[t, c], rsp_send.at[t, c], rsp_recv.at[t, c], up
        )

    def rs_down(t, c):
        return remote(
            rs_send_m.at[t, c], rs_recv_m.at[t, c], rsm_send.at[t, c], rsm_recv.at[t, c], down
        )

    def rs_step(t, c):
        if t < DOWN:
            value = piece(c, z - DOWN + t)
            if t > 0:
                rs_down(t - 1, c).wait_recv()
                value = value + rs_recv_m[t - 1, c].astype(f32)
            rs_send_m[t, c] = value.astype(bf16)
            rs_down(t, c).start()
        if t < UP:
            value = piece(c, z + UP - t)
            if t > 0:
                rs_up(t - 1, c).wait_recv()
                value = value + rs_recv_p[t - 1, c].astype(f32)
            rs_send_p[t, c] = value.astype(bf16)
            rs_up(t, c).start()

    grad[2] = dot_n(activation, values)
    rs_step(0, 2)
    window_step(0)
    grad[1] = dot_n(grad_up, keys)
    rs_step(0, 1)
    window_step(1)
    grad[0] = dot_n(grad_gate, keys)
    rs_step(0, 0)
    loads[3].wait()

    exponent = math.log2(math.e) / math.sqrt(D)
    HALF = T // 2

    def attend(d, kh, qh):
        span = pl.ds(qh * HALF, HALF)
        part = pl.ds(kh * HALF, HALF)
        scores = dot_t(q[span, :], kv[d, 0, part, :])
        if d in (0, Y):
            behind = (
                lax.broadcasted_iota(jnp.int32, (HALF, HALF), 0)
                - lax.broadcasted_iota(jnp.int32, (HALF, HALF), 1)
                + ((qh - kh) * HALF + d * T)
            )
            scores = jnp.where((behind >= 0) & (behind < WIN), scores, -jnp.inf)
        if d > 0:
            scores = scores + jnp.where(s >= d, 0.0, -jnp.inf)
        peak = jnp.max(scores, axis=1, keepdims=True)
        if d == 0 and kh == 0:
            expo = jnp.exp2((scores - peak) * exponent)
            row_l[span, :] = jnp.broadcast_to(jnp.sum(expo, axis=1, keepdims=True), (HALF, 128))
            acc[span, :] = dot_n(expo.astype(bf16), kv[d, 1, part, :])
        else:
            before = row_m[span, :][:, 0:1]
            peak = jnp.maximum(before, peak)
            decay = jnp.exp2((before - peak) * exponent)
            expo = jnp.exp2((scores - peak) * exponent)
            row_l[span, :] = row_l[span, :] * decay + jnp.sum(expo, axis=1, keepdims=True)
            acc[span, :] = acc[span, :] * decay + dot_n(expo.astype(bf16), kv[d, 1, part, :])
        row_m[span, :] = jnp.broadcast_to(peak, (HALF, 128))

    def swiglu(inputs, gate_w, up_w, down_w):
        gate = dot_t(inputs, gate_w)
        hidden = (gate * jax.nn.sigmoid(gate) * dot_t(inputs, up_w)).astype(bf16)
        return dot_n(hidden, down_w).astype(bf16)

    def early_fast(part):
        span = pl.ds(part * (T // 4), T // 4)
        first_out[span, :] = swiglu(q[span, :], w[0], w[1], w[2])

    fillers = [functools.partial(attend, 0, 0, qh) for qh in range(2)]
    fillers += [functools.partial(attend, 0, 1, qh) for qh in range(1, 2)]
    fillers += [functools.partial(early_fast, part) for part in range(4)]
    steps = max(UP, DOWN)
    seen = 2
    for t in range(1, steps):
        for c in (2, 1, 0):
            rs_step(t, c)
        window_step(seen)
        seen += 1
        if fillers:
            fillers.pop(0)()

    def y_copy(k, c):
        return remote(
            y_send.at[c], y_recv.at[k - 1, c], ys_send.at[k - 1, c], ys_recv.at[k - 1, c],
            seq_at(z, y + k),
        )

    for c in (2, 1, 0):
        value = piece(c, z)
        if DOWN > 0:
            rs_down(DOWN - 1, c).wait_recv()
            value = value + rs_recv_m[DOWN - 1, c].astype(f32)
        rs_up(UP - 1, c).wait_recv()
        value = value + rs_recv_p[UP - 1, c].astype(f32)
        total[c] = value
        y_send[c] = value.astype(bf16)
        for k in range(1, Y):
            y_copy(k, c).start()
    while fillers:
        fillers.pop(0)()

    def idx_body(k, carry):
        target = lax.rem(s + k, N)
        remote(wanted.at[target], asked.at[s], idx_send, idx_recv, target).start()
        return carry

    group_count = jnp.full((1, D), first_len, jnp.int32).astype(f32)
    rate = lr_ref[0] / group_count
    for c in (2, 1, 0):
        value = total[c]
        for k in range(1, Y):
            y_copy(k, c).wait_recv()
            value = value + y_recv[k - 1, c].astype(f32)
        previous = w[c, pl.ds(pl.multiple_of(z * FR, FR), FR), :].astype(f32)
        updated = previous + rate * value
        old_norm = jnp.sqrt(jnp.sum(previous * previous, axis=1, keepdims=True) + eps)
        new_norm = jnp.sqrt(jnp.sum(updated * updated, axis=1, keepdims=True) + eps)
        new_w[z, c] = (updated * (old_norm / new_norm)).astype(bf16)

    def ag_up(t, c):
        at = chunk_of(z - t)
        return remote(new_w.at[at, c], new_w.at[at, c], agp_send.at[t, c], agp_recv.at[t, c], up)

    def ag_down(t, c):
        at = chunk_of(z + t)
        return remote(new_w.at[at, c], new_w.at[at, c], agm_send.at[t, c], agm_recv.at[t, c], down)

    def ag_wait_up(t, c):
        at = chunk_of(z - 1 - t)
        remote(
            new_w.at[at, c], new_w.at[at, c], agp_send.at[t, c], agp_recv.at[t, c], up
        ).wait_recv()

    def ag_wait_down(t, c):
        at = chunk_of(z + 1 + t)
        remote(
            new_w.at[at, c], new_w.at[at, c], agm_send.at[t, c], agm_recv.at[t, c], down
        ).wait_recv()

    def block_ready(d, kh):
        for i in range(kh * CHUNKS // 2, (kh + 1) * CHUNKS // 2):
            if d == 2:
                for j in range(2):
                    forward(j, i).wait_recv()
            elif d != Y:
                spread(d, i).wait_recv()

    def block(d, kh, qh):
        if qh == 0:
            block_ready(d, kh)
        attend(d, kh, qh)

    fillers = [
        functools.partial(block, d, kh, qh)
        for kh in range(2) for d in (Y, 1, 3, 2) for qh in range(2)
        if (d, kh, qh) != (Y, 0, 1)
    ]
    for t in range(steps):
        for c in (2, 1, 0):
            if t < DOWN:
                if t > 0:
                    ag_wait_down(t - 1, c)
                ag_down(t, c).start()
            if t < UP:
                if t > 0:
                    ag_wait_up(t - 1, c)
                ag_up(t, c).start()
        if t == 0:
            lax.fori_loop(1, N, idx_body, 0)
            asked[s] = wanted[s]
        if seen <= CHUNKS:
            window_step(seen)
            seen += 1
        for _ in range(1 if t < 6 else 2):
            if fillers and seen > (CHUNKS if len(fillers) <= 8 else CHUNKS // 2):
                fillers.pop(0)()
    while seen <= CHUNKS:
        window_step(seen)
        seen += 1
    while fillers:
        fillers.pop(0)()
    pltpu.make_async_copy(asked.at[pl.ds(0, N - 1)], asked.at[pl.ds(0, N - 1)], idx_recv).wait()
    attention = (acc[...] / row_l[...][:, 0:1]).astype(bf16)
    lines = jnp.broadcast_to(asked[...].astype(f32), (N, SEG, 128)).reshape(T, 128)
    lane = lax.broadcasted_iota(jnp.int32, (T, 128), 1)
    spot = lax.rem(lax.broadcasted_iota(jnp.int32, (T, 128), 0), SEG)
    picked = jnp.sum(jnp.where(lane == spot, lines, 0.0), axis=1, keepdims=True)
    column = lax.broadcasted_iota(jnp.int32, (T, T), 1).astype(f32)
    choose[...] = jnp.where(column == picked, 1.0, 0.0).astype(bf16)
    rows[...] = dot_n(choose[...], attention)
    for c in (2, 1, 0):
        if DOWN > 0:
            ag_wait_down(DOWN - 1, c)
        ag_wait_up(UP - 1, c)

    second = swiglu(
        q[...], new_w[:, 0].reshape(F, D), new_w[:, 1].reshape(F, D), new_w[:, 2].reshape(F, D)
    )
    member = (s * T + lax.broadcasted_iota(jnp.int32, (T, D), 0)) < first_len
    fast = jnp.where(member, first_out[...].astype(f32), second.astype(f32))
    summed = attention.astype(f32) + fast
    square = summed * summed
    coarse = square.astype(bf16)
    fine = (square - coarse.astype(f32)).astype(bf16)
    ones = jnp.ones((8, D), bf16)
    power[h] = (dot_t(ones, coarse) + dot_t(ones, fine))[0:1, :]

    def pow_copy(k):
        return pltpu.make_async_remote_copy(
            src_ref=power.at[h], dst_ref=power.at[h],
            send_sem=pow_send.at[k - 1], recv_sem=pow_recv.at[k - 1],
            device_id={"head": lax.rem(h + k, H)}, device_id_type=MESH,
        )

    for k in range(1, H):
        pow_copy(k).start()
    rows[...] = rows[...] + dot_n(choose[...], fast.astype(bf16))
    for k in range(1, H):
        pow_copy(k).wait_recv()
    strength = power[0]
    for k in range(1, H):
        strength = strength + power[k]
    row_scale = lax.rsqrt(strength / (H * D) + eps)

    GROUPS = 4
    NG = N // GROUPS
    TG = T // GROUPS
    for far in (2, 1, 3, 0):
        g = lax.rem(s // NG + far, GROUPS)
        span = pl.ds(pl.multiple_of(g * TG, TG), TG)
        factor = jnp.sum(choose[span, :].astype(f32) * row_scale, axis=1, keepdims=True)
        normed = rows[span, :] * factor * gain_ref[...]
        send_rows[pl.ds(g * NG, NG)] = normed.reshape(NG, SEG, D).astype(bf16)

        def a2a_body(k, carry):
            target = g * NG + k

            @pl.when(target != s)
            def _():
                remote(send_rows.at[target], out_ref.at[s], a2a_send, a2a_recv, target).start()

            return carry

        lax.fori_loop(0, NG, a2a_body, 0)
    own = pltpu.make_async_copy(send_rows.at[s], out_ref.at[s], own_sem)
    own.start()

    for i in range(CHUNKS):
        zhop(i).wait_send()
        spread(1, i).wait_send()
        spread(3, i).wait_send()
        for j in range(2):
            over(j, i).wait_send()
            forward(j, i).wait_send()
    for c in range(3):
        for t in range(UP):
            rs_up(t, c).wait_send()
            ag_up(t, c).wait_send()
        for t in range(DOWN):
            rs_down(t, c).wait_send()
            ag_down(t, c).wait_send()
        for k in range(1, Y):
            y_copy(k, c).wait_send()
    for k in range(1, H):
        pow_copy(k).wait_send()
    pltpu.make_async_copy(wanted.at[pl.ds(0, N - 1)], wanted.at[pl.ds(0, N - 1)], idx_send).wait()
    own.wait()
    pltpu.make_async_copy(
        send_rows.at[pl.ds(0, N - 1)], send_rows.at[pl.ds(0, N - 1)], a2a_send
    ).wait()
    pltpu.make_async_copy(
        out_ref.at[pl.ds(0, N - 1)], out_ref.at[pl.ds(0, N - 1)], a2a_recv
    ).wait()


def solution(mesh, window=WINDOW):
    N = mesh.shape["seq"]
    H = mesh.shape["head"]

    def per_device(q, k, v, weights, learn_rate, out_gain, group_lengths, slot_order):
        T, _, D = q.shape
        F = weights.shape[0]
        Y = window // T
        Z = N // Y
        UP = min(UP_HOPS, Z // 2)
        DOWN = Z - 1 - UP
        FR = F // Z
        SEG = T // N
        dma = pltpu.SemaphoreType.DMA
        VMEM = pltpu.VMEM
        any_spec = pl.BlockSpec(memory_space=pl.ANY)
        vmem_spec = pl.BlockSpec(memory_space=pltpu.VMEM)
        smem_spec = pl.BlockSpec(memory_space=pltpu.SMEM)
        out = pl.pallas_call(
            functools.partial(layer_kernel, Y, Z, H, UP, DOWN, window),
            out_shape=jax.ShapeDtypeStruct((N, SEG, D), bf16),
            in_specs=[any_spec] * 4 + [smem_spec, vmem_spec, smem_spec, vmem_spec],
            out_specs=any_spec,
            scratch_shapes=[
                VMEM((T, D), bf16),
                VMEM((Y + 1, 2, T, D), bf16),
                VMEM((3, F, D), bf16),
                VMEM((2, T, D), bf16),
                VMEM((3, F, D), f32),
                VMEM((UP, 3, FR, D), bf16),
                VMEM((max(DOWN, 1), 3, FR, D), bf16),
                VMEM((UP, 3, FR, D), bf16),
                VMEM((max(DOWN, 1), 3, FR, D), bf16),
                VMEM((3, FR, D), f32),
                VMEM((3, FR, D), bf16),
                VMEM((Y - 1, 3, FR, D), bf16),
                VMEM((Z, 3, FR, D), bf16),
                VMEM((T, D), f32),
                VMEM((T, 128), f32),
                VMEM((T, 128), f32),
                VMEM((T, D), bf16),
                VMEM((T, D), f32),
                VMEM((H, 1, T), f32),
                VMEM((N, 1, 128), jnp.int32),
                VMEM((N, 1, 128), jnp.int32),
                VMEM((T, T), bf16),
                VMEM((N, SEG, D), bf16),
                dma((4,)),
                dma((Y + 1, CHUNKS)),
                dma((Y + 1, CHUNKS)),
                dma((2, CHUNKS)),
                dma((2, CHUNKS)),
                dma((2, CHUNKS)),
                dma((2, CHUNKS)),
                dma((UP, 3)),
                dma((UP, 3)),
                dma((max(DOWN, 1), 3)),
                dma((max(DOWN, 1), 3)),
                dma((Y - 1, 3)),
                dma((Y - 1, 3)),
                dma((UP, 3)),
                dma((UP, 3)),
                dma((max(DOWN, 1), 3)),
                dma((max(DOWN, 1), 3)),
                dma((max(H - 1, 1),)),
                dma((max(H - 1, 1),)),
                dma,
                dma,
                dma,
                dma,
                dma,
            ],
            compiler_params=pltpu.CompilerParams(
                collective_id=0, has_side_effects=True, vmem_limit_bytes=60 * 1024 * 1024
            ),
            name="ttt_layer",
        )(
            q.reshape(T, D), k.reshape(T, D), v.reshape(T, D),
            jnp.transpose(weights.reshape(F, 3, D), (1, 0, 2)),
            learn_rate, out_gain, group_lengths, slot_order.reshape(T // 128, 128),
        )
        return out.reshape(T, 1, D)

    return jax.shard_map(
        per_device,
        mesh=mesh,
        in_specs=(
            P("seq", "head", None),
            P("seq", "head", None),
            P("seq", "head", None),
            P(None, "head", None, None),
            P("head"),
            P("head", None),
            P(),
            P("seq"),
        ),
        out_specs=P("seq", "head", None),
        check_vma=False,
    )
```

```python
import functools
import math

import jax
import jax.numpy as jnp
from jax import lax
from jax.experimental import pallas as pl
from jax.experimental.pallas import tpu as pltpu
from jax.sharding import PartitionSpec as P

WINDOW = 2048
CHUNKS = 16
UP_HOPS = 7
SUB = 1
eps = 1e-06
MESH = pl.DeviceIdType.MESH
f32 = jnp.float32
bf16 = jnp.bfloat16


def dot_t(a, b):
    return lax.dot_general(a, b, (((1,), (1,)), ((), ())), preferred_element_type=f32)


def dot_n(a, b):
    return jnp.dot(a, b, preferred_element_type=f32)


def layer_kernel(
    Y, Z, H, UP, DOWN, WIN,
    q_hbm, k_hbm, v_hbm, w_hbm, lr_ref, gain_ref, len_ref, slot_ref,
    out_ref,
    q, kv, w, relay, grad, rs_send_p, rs_send_m, rs_recv_p, rs_recv_m,
    total, y_send, y_recv, new_w, acc, row_m, row_l, first_out, rows,
    power, wanted, asked, choose, send_rows,
    load_sem, win_send, win_recv, relay_send, relay_recv, fwd_send, mid_recv,
    rsp_send, rsp_recv, rsm_send, rsm_recv, ys_send, ys_recv,
    agp_send, agp_recv, agm_send, agm_recv,
    pow_send, pow_recv, idx_send, idx_recv, a2a_send, a2a_recv, own_sem,
):
    T, D = q.shape
    F = w.shape[1]
    FR = F // Z
    N = Y * Z
    SEG = T // N
    CR = T // CHUNKS
    s = lax.axis_index("seq")
    h = lax.axis_index("head")
    z = s // Y
    y = s % Y

    def seq_at(zz, yy):
        return lax.rem(zz + Z, Z) * Y + lax.rem(yy + Y, Y)

    up = seq_at(z + 1, y)
    down = seq_at(z - 1, y)

    def remote(src, dst, ssem, rsem, seq):
        return pltpu.make_async_remote_copy(
            src_ref=src, dst_ref=dst, send_sem=ssem, recv_sem=rsem,
            device_id={"seq": seq}, device_id_type=MESH,
        )

    loads = [
        pltpu.make_async_copy(k_hbm, kv.at[0, 0], load_sem.at[0]),
        pltpu.make_async_copy(v_hbm, kv.at[0, 1], load_sem.at[1]),
        pltpu.make_async_copy(w_hbm, w, load_sem.at[2]),
        pltpu.make_async_copy(q_hbm, q, load_sem.at[3]),
    ]
    for copy in loads:
        copy.start()

    barrier = pltpu.get_barrier_semaphore()
    near = [up, down] + [seq_at(z, y + k) for k in range(1, Y)]
    for partner in near:
        pl.semaphore_signal(barrier, inc=1, device_id={"seq": partner}, device_id_type=MESH)
    for k in range(1, H):
        pl.semaphore_signal(
            barrier, inc=1, device_id={"head": lax.rem(h + k, H)}, device_id_type=MESH
        )
    for g in range(128 // SEG):
        line = slot_ref[...] if g == 0 else pltpu.roll(slot_ref[...], 128 - SEG * g, 1)
        for i in range(T // 128):
            e = i * (128 // SEG) + g
            wanted[e] = line[i : i + 1, :] - e * T
    pl.semaphore_wait(barrier, len(near) + H - 1)
    loads[0].wait()
    loads[1].wait()

    def rows_of(i):
        return pl.ds(i * CR, CR)

    def zhop(i):
        return remote(
            kv.at[0, :, rows_of(i)], kv.at[Y, :, rows_of(i)],
            win_send.at[Y, i], win_recv.at[Y, i], up,
        )

    def spread(k, i):
        src = jnp.where(y + k < Y, 0, Y)
        return remote(
            kv.at[src, :, rows_of(i)], kv.at[k, :, rows_of(i)],
            win_send.at[k, i], win_recv.at[k, i], seq_at(z, y + k),
        )

    def over(j, i):
        src = jnp.where(y + 2 < Y, 0, Y)
        return remote(
            kv.at[src, j, rows_of(i)], relay.at[j, rows_of(i)],
            relay_send.at[j, i], relay_recv.at[j, i], seq_at(z, y + (1 if j == 0 else -1)),
        )

    def forward(j, i):
        return remote(
            relay.at[j, rows_of(i)], kv.at[2, j, rows_of(i)],
            fwd_send.at[j, i], mid_recv.at[j, i], seq_at(z, y + (1 if j == 0 else -1)),
        )

    AHEAD = 3
    for i in range(AHEAD):
        zhop(i).start()

    def window_step(i):
        if i < CHUNKS:
            if i + AHEAD < CHUNKS:
                zhop(i + AHEAD).start()
            zhop(i).wait_recv()
            for j in range(2):
                over(j, i).start()
            spread(1, i).start()
            spread(3, i).start()
        if 1 <= i <= CHUNKS:
            for j in range(2):
                over(j, i - 1).wait_recv()
                forward(j, i - 1).start()

    first_len = len_ref[0]
    lane_member = (s * T + lax.broadcasted_iota(jnp.int32, (1, T), 1)) < first_len
    loads[2].wait()
    keys = kv[0, 0]
    values = kv[0, 1]
    gate_pre = dot_t(w[0], keys)
    up_pre = dot_t(w[1], keys)
    sig_gate = jax.nn.sigmoid(gate_pre)
    gated = gate_pre * sig_gate
    activation = jnp.where(lane_member, gated * up_pre, 0.0).astype(bf16)
    back = jnp.where(lane_member, dot_t(w[2], values), 0.0)
    grad_up = (back * gated).astype(bf16)
    grad_gate = (back * up_pre * sig_gate * (1.0 + gate_pre * (1.0 - sig_gate))).astype(bf16)

    def chunk_of(zz):
        return lax.rem(zz + 2 * Z, Z)

    HR = FR // SUB
    units = [(c, b) for c in (2, 1, 0) for b in range(SUB)]

    def at_rows(u):
        return pl.ds(u[1] * HR, HR)

    def slot(u):
        return u[0] * SUB + u[1]

    def piece(u, zz):
        first = pl.multiple_of(chunk_of(zz) * FR + u[1] * HR, HR)
        return grad[u[0], pl.ds(first, HR), :]

    def rs_up(t, u):
        return remote(
            rs_send_p.at[t, u[0], at_rows(u)], rs_recv_p.at[t, u[0], at_rows(u)],
            rsp_send.at[t, slot(u)], rsp_recv.at[t, slot(u)], up,
        )

    def rs_down(t, u):
        return remote(
            rs_send_m.at[t, u[0], at_rows(u)], rs_recv_m.at[t, u[0], at_rows(u)],
            rsm_send.at[t, slot(u)], rsm_recv.at[t, slot(u)], down,
        )

    def rs_step(t, u):
        if t < DOWN:
            value = piece(u, z - DOWN + t)
            if t > 0:
                rs_down(t - 1, u).wait_recv()
                value = value + rs_recv_m[t - 1, u[0], at_rows(u)].astype(f32)
            rs_send_m[t, u[0], at_rows(u)] = value.astype(bf16)
            rs_down(t, u).start()
        if t < UP:
            value = piece(u, z + UP - t)
            if t > 0:
                rs_up(t - 1, u).wait_recv()
                value = value + rs_recv_p[t - 1, u[0], at_rows(u)].astype(f32)
            rs_send_p[t, u[0], at_rows(u)] = value.astype(bf16)
            rs_up(t, u).start()

    grad[2] = dot_n(activation, values)
    for b in range(SUB):
        rs_step(0, (2, b))
    window_step(0)
    grad[1] = dot_n(grad_up, keys)
    for b in range(SUB):
        rs_step(0, (1, b))
    window_step(1)
    grad[0] = dot_n(grad_gate, keys)
    for b in range(SUB):
        rs_step(0, (0, b))
    loads[3].wait()

    exponent = math.log2(math.e) / math.sqrt(D)
    HALF = T // 2

    def attend(d, kh, qh):
        span = pl.ds(qh * HALF, HALF)
        part = pl.ds(kh * HALF, HALF)
        scores = dot_t(q[span, :], kv[d, 0, part, :])
        if d in (0, Y):
            behind = (
                lax.broadcasted_iota(jnp.int32, (HALF, HALF), 0)
                - lax.broadcasted_iota(jnp.int32, (HALF, HALF), 1)
                + ((qh - kh) * HALF + d * T)
            )
            scores = jnp.where((behind >= 0) & (behind < WIN), scores, -jnp.inf)
        if d > 0:
            scores = scores + jnp.where(s >= d, 0.0, -jnp.inf)
        peak = jnp.max(scores, axis=1, keepdims=True)
        if d == 0 and kh == 0:
            expo = jnp.exp2((scores - peak) * exponent)
            row_l[span, :] = jnp.broadcast_to(jnp.sum(expo, axis=1, keepdims=True), (HALF, 128))
            acc[span, :] = dot_n(expo.astype(bf16), kv[d, 1, part, :])
        else:
            before = row_m[span, :][:, 0:1]
            peak = jnp.maximum(before, peak)
            decay = jnp.exp2((before - peak) * exponent)
            expo = jnp.exp2((scores - peak) * exponent)
            row_l[span, :] = row_l[span, :] * decay + jnp.sum(expo, axis=1, keepdims=True)
            acc[span, :] = acc[span, :] * decay + dot_n(expo.astype(bf16), kv[d, 1, part, :])
        row_m[span, :] = jnp.broadcast_to(peak, (HALF, 128))

    def swiglu(inputs, gate_w, up_w, down_w):
        gate = dot_t(inputs, gate_w)
        hidden = (gate * jax.nn.sigmoid(gate) * dot_t(inputs, up_w)).astype(bf16)
        return dot_n(hidden, down_w).astype(bf16)

    def early_fast(part):
        span = pl.ds(part * (T // 4), T // 4)
        first_out[span, :] = swiglu(q[span, :], w[0], w[1], w[2])

    fillers = [functools.partial(attend, 0, 0, qh) for qh in range(2)]
    fillers += [functools.partial(attend, 0, 1, 1)]
    fillers += [functools.partial(early_fast, part) for part in range(4)]
    steps = max(UP, DOWN)
    seen = 2
    for t in range(1, steps):
        for u in units:
            rs_step(t, u)
        window_step(seen)
        seen += 1
        if fillers:
            fillers.pop(0)()

    def y_copy(k, c):
        return remote(
            y_send.at[c], y_recv.at[k - 1, c], ys_send.at[k - 1, c], ys_recv.at[k - 1, c],
            seq_at(z, y + k),
        )

    for c in (2, 1, 0):
        for b in range(SUB):
            u = (c, b)
            value = piece(u, z)
            rs_down(DOWN - 1, u).wait_recv()
            value = value + rs_recv_m[DOWN - 1, c, at_rows(u)].astype(f32)
            rs_up(UP - 1, u).wait_recv()
            total[c, at_rows(u)] = value + rs_recv_p[UP - 1, c, at_rows(u)].astype(f32)
        value = total[c]
        y_send[c] = value.astype(bf16)
        for k in range(1, Y):
            y_copy(k, c).start()
    while fillers:
        fillers.pop(0)()

    def idx_body(k, carry):
        target = lax.rem(s + k, N)
        remote(wanted.at[target], asked.at[s], idx_send, idx_recv, target).start()
        return carry

    group_count = jnp.full((1, D), first_len, jnp.int32).astype(f32)
    rate = lr_ref[0] / group_count
    for c in (2, 1, 0):
        value = total[c]
        for k in range(1, Y):
            y_copy(k, c).wait_recv()
            value = value + y_recv[k - 1, c].astype(f32)
        previous = w[c, pl.ds(pl.multiple_of(z * FR, FR), FR), :].astype(f32)
        updated = previous + rate * value
        old_norm = jnp.sqrt(jnp.sum(previous * previous, axis=1, keepdims=True) + eps)
        new_norm = jnp.sqrt(jnp.sum(updated * updated, axis=1, keepdims=True) + eps)
        new_w[z, c] = (updated * (old_norm / new_norm)).astype(bf16)

    def ag_copy(at, t, u, ssem, rsem, seq):
        part = new_w.at[at, u[0], at_rows(u)]
        return remote(part, part, ssem.at[t, slot(u)], rsem.at[t, slot(u)], seq)

    def ag_up(t, u):
        return ag_copy(chunk_of(z - t), t, u, agp_send, agp_recv, up)

    def ag_down(t, u):
        return ag_copy(chunk_of(z + t), t, u, agm_send, agm_recv, down)

    def ag_wait_up(t, u):
        ag_copy(chunk_of(z - 1 - t), t, u, agp_send, agp_recv, up).wait_recv()

    def ag_wait_down(t, u):
        ag_copy(chunk_of(z + 1 + t), t, u, agm_send, agm_recv, down).wait_recv()

    def block_ready(d, kh):
        for i in range(kh * CHUNKS // 2, (kh + 1) * CHUNKS // 2):
            if d == 2:
                for j in range(2):
                    forward(j, i).wait_recv()
            elif d != Y:
                spread(d, i).wait_recv()

    def block(d, kh, qh):
        if qh == 0:
            block_ready(d, kh)
        attend(d, kh, qh)

    fillers = [
        functools.partial(block, d, kh, qh)
        for kh in range(2) for d in (Y, 1, 3, 2) for qh in range(2)
        if (d, kh, qh) != (Y, 0, 1)
    ]
    def find_rows():
        pltpu.make_async_copy(
            asked.at[pl.ds(0, N - 1)], asked.at[pl.ds(0, N - 1)], idx_recv
        ).wait()
        lines = jnp.broadcast_to(asked[...].astype(f32), (N, SEG, 128)).reshape(T, 128)
        lane = lax.broadcasted_iota(jnp.int32, (T, 128), 1)
        spot = lax.rem(lax.broadcasted_iota(jnp.int32, (T, 128), 0), SEG)
        picked = jnp.sum(jnp.where(lane == spot, lines, 0.0), axis=1, keepdims=True)
        column = lax.broadcasted_iota(jnp.int32, (T, T), 1).astype(f32)
        choose[...] = jnp.where(column == picked, 1.0, 0.0).astype(bf16)

    near_set = list(range(-((Z // 2) // 2), (Z // 2) - (Z // 2) // 2))
    far_set = [o for o in range(-UP, DOWN + 1) if o not in near_set]

    def partial_fast(offsets):
        gate_w, up_w, down_w = (
            jnp.concatenate([new_w[chunk_of(z + o), c] for o in offsets], axis=0) for c in range(3)
        )
        gate = dot_t(q[...], gate_w)
        hidden = (gate * jax.nn.sigmoid(gate) * dot_t(q[...], up_w)).astype(bf16)
        return dot_n(hidden, down_w)

    def near_fast():
        rows[...] = partial_fast(near_set)

    extra = [find_rows]
    for t in range(steps):
        for u in units:
            if t < DOWN:
                if t > 0:
                    ag_wait_down(t - 1, u)
                ag_down(t, u).start()
            if t < UP:
                if t > 0:
                    ag_wait_up(t - 1, u)
                ag_up(t, u).start()
        if t == 0:
            lax.fori_loop(1, N, idx_body, 0)
            asked[s] = wanted[s]
        for _ in range(1):
            if seen <= CHUNKS:
                window_step(seen)
                seen += 1
        for _ in range(2):
            if fillers and seen > (CHUNKS if len(fillers) <= 8 else CHUNKS // 2):
                fillers.pop(0)()
        if t == steps - 3:
            find_rows()
            extra.clear()
    while seen <= CHUNKS:
        window_step(seen)
        seen += 1
    while fillers:
        fillers.pop(0)()
    for step in extra:
        step()
    if steps <= 2:
        for u in units:
            ag_wait_down(DOWN - 1, u)
            ag_wait_up(UP - 1, u)
    near_fast()
    attention = (acc[...] / row_l[...][:, 0:1]).astype(bf16)
    acc[...] = dot_n(choose[...], attention)
    if steps > 2:
        for u in units:
            ag_wait_down(DOWN - 1, u)
            ag_wait_up(UP - 1, u)

    second = (rows[...] + partial_fast(far_set)).astype(bf16)
    member = (s * T + lax.broadcasted_iota(jnp.int32, (T, D), 0)) < first_len
    fast = jnp.where(member, first_out[...].astype(f32), second.astype(f32))
    summed = attention.astype(f32) + fast
    square = summed * summed
    coarse = square.astype(bf16)
    fine = (square - coarse.astype(f32)).astype(bf16)
    ones = jnp.ones((8, D), bf16)
    power[h] = (dot_t(ones, coarse) + dot_t(ones, fine))[0:1, :]

    def pow_copy(k):
        return pltpu.make_async_remote_copy(
            src_ref=power.at[h], dst_ref=power.at[h],
            send_sem=pow_send.at[k - 1], recv_sem=pow_recv.at[k - 1],
            device_id={"head": lax.rem(h + k, H)}, device_id_type=MESH,
        )

    for k in range(1, H):
        pow_copy(k).start()
    rows[...] = acc[...] + dot_n(choose[...], fast.astype(bf16))
    for k in range(1, H):
        pow_copy(k).wait_recv()
    strength = power[0]
    for k in range(1, H):
        strength = strength + power[k]
    row_scale = lax.rsqrt(strength / (H * D) + eps)

    GROUPS = 4
    NG = N // GROUPS
    TG = T // GROUPS
    for far in (2, 1, 3, 0):
        g = lax.rem(s // NG + far, GROUPS)
        span = pl.ds(pl.multiple_of(g * TG, TG), TG)
        factor = jnp.sum(choose[span, :].astype(f32) * row_scale, axis=1, keepdims=True)
        normed = rows[span, :] * factor * gain_ref[...]
        send_rows[pl.ds(g * NG, NG)] = normed.reshape(NG, SEG, D).astype(bf16)

        def a2a_body(k, carry):
            target = g * NG + k

            @pl.when(target != s)
            def _():
                remote(send_rows.at[target], out_ref.at[s], a2a_send, a2a_recv, target).start()

            return carry

        lax.fori_loop(0, NG, a2a_body, 0)
    own = pltpu.make_async_copy(send_rows.at[s], out_ref.at[s], own_sem)
    own.start()

    for i in range(CHUNKS):
        zhop(i).wait_send()
        spread(1, i).wait_send()
        spread(3, i).wait_send()
        for j in range(2):
            over(j, i).wait_send()
            forward(j, i).wait_send()
    for u in units:
        for t in range(UP):
            rs_up(t, u).wait_send()
            ag_up(t, u).wait_send()
        for t in range(DOWN):
            rs_down(t, u).wait_send()
            ag_down(t, u).wait_send()
    for c in range(3):
        for k in range(1, Y):
            y_copy(k, c).wait_send()
    for k in range(1, H):
        pow_copy(k).wait_send()
    pltpu.make_async_copy(wanted.at[pl.ds(0, N - 1)], wanted.at[pl.ds(0, N - 1)], idx_send).wait()
    own.wait()
    pltpu.make_async_copy(
        send_rows.at[pl.ds(0, N - 1)], send_rows.at[pl.ds(0, N - 1)], a2a_send
    ).wait()
    pltpu.make_async_copy(
        out_ref.at[pl.ds(0, N - 1)], out_ref.at[pl.ds(0, N - 1)], a2a_recv
    ).wait()


def solution(mesh, window=WINDOW):
    N = mesh.shape["seq"]
    H = mesh.shape["head"]

    def per_device(q, k, v, weights, learn_rate, out_gain, group_lengths, slot_order):
        T, _, D = q.shape
        F = weights.shape[0]
        Y = window // T
        Z = N // Y
        UP = min(UP_HOPS, Z // 2)
        DOWN = Z - 1 - UP
        FR = F // Z
        SEG = T // N
        dma = pltpu.SemaphoreType.DMA
        VMEM = pltpu.VMEM
        any_spec = pl.BlockSpec(memory_space=pl.ANY)
        vmem_spec = pl.BlockSpec(memory_space=pltpu.VMEM)
        smem_spec = pl.BlockSpec(memory_space=pltpu.SMEM)
        out = pl.pallas_call(
            functools.partial(layer_kernel, Y, Z, H, UP, DOWN, window),
            out_shape=jax.ShapeDtypeStruct((N, SEG, D), bf16),
            in_specs=[any_spec] * 4 + [smem_spec, vmem_spec, smem_spec, vmem_spec],
            out_specs=any_spec,
            scratch_shapes=[
                VMEM((T, D), bf16),
                VMEM((Y + 1, 2, T, D), bf16),
                VMEM((3, F, D), bf16),
                VMEM((2, T, D), bf16),
                VMEM((3, F, D), f32),
                VMEM((UP, 3, FR, D), bf16),
                VMEM((max(DOWN, 1), 3, FR, D), bf16),
                VMEM((UP, 3, FR, D), bf16),
                VMEM((max(DOWN, 1), 3, FR, D), bf16),
                VMEM((3, FR, D), f32),
                VMEM((3, FR, D), bf16),
                VMEM((Y - 1, 3, FR, D), bf16),
                VMEM((Z, 3, FR, D), bf16),
                VMEM((T, D), f32),
                VMEM((T, 128), f32),
                VMEM((T, 128), f32),
                VMEM((T, D), bf16),
                VMEM((T, D), f32),
                VMEM((H, 1, T), f32),
                VMEM((N, 1, 128), jnp.int32),
                VMEM((N, 1, 128), jnp.int32),
                VMEM((T, T), bf16),
                VMEM((N, SEG, D), bf16),
                dma((4,)),
                dma((Y + 1, CHUNKS)),
                dma((Y + 1, CHUNKS)),
                dma((2, CHUNKS)),
                dma((2, CHUNKS)),
                dma((2, CHUNKS)),
                dma((2, CHUNKS)),
                dma((UP, 3 * SUB)),
                dma((UP, 3 * SUB)),
                dma((max(DOWN, 1), 3 * SUB)),
                dma((max(DOWN, 1), 3 * SUB)),
                dma((Y - 1, 3)),
                dma((Y - 1, 3)),
                dma((UP, 3 * SUB)),
                dma((UP, 3 * SUB)),
                dma((max(DOWN, 1), 3 * SUB)),
                dma((max(DOWN, 1), 3 * SUB)),
                dma((max(H - 1, 1),)),
                dma((max(H - 1, 1),)),
                dma,
                dma,
                dma,
                dma,
                dma,
            ],
            compiler_params=pltpu.CompilerParams(
                collective_id=0, has_side_effects=True, vmem_limit_bytes=60 * 1024 * 1024
            ),
            name="ttt_layer",
        )(
            q.reshape(T, D), k.reshape(T, D), v.reshape(T, D),
            jnp.transpose(weights.reshape(F, 3, D), (1, 0, 2)),
            learn_rate, out_gain, group_lengths, slot_order.reshape(T // 128, 128),
        )
        return out.reshape(T, 1, D)

    return jax.shard_map(
        per_device,
        mesh=mesh,
        in_specs=(
            P("seq", "head", None),
            P("seq", "head", None),
            P("seq", "head", None),
            P(None, "head", None, None),
            P("head"),
            P("head", None),
            P(),
            P("seq"),
        ),
        out_specs=P("seq", "head", None),
        check_vma=False,
    )
```

```python
import functools
import math

import jax
import jax.numpy as jnp
from jax import lax
from jax.experimental import pallas as pl
from jax.experimental.pallas import tpu as pltpu
from jax.sharding import PartitionSpec as P

WINDOW = 2048
CHUNKS = 16
UP_HOPS = 7
SUB = 1
eps = 1e-06
MESH = pl.DeviceIdType.MESH
f32 = jnp.float32
bf16 = jnp.bfloat16


def dot_t(a, b):
    return lax.dot_general(a, b, (((1,), (1,)), ((), ())), preferred_element_type=f32)


def dot_n(a, b):
    return jnp.dot(a, b, preferred_element_type=f32)


def layer_kernel(
    Y, Z, H, UP, DOWN, WIN,
    q_hbm, k_hbm, v_hbm, w_hbm, lr_ref, gain_ref, len_ref, slot_ref,
    out_ref,
    q, kv, w, relay, grad, rs_send_p, rs_send_m, rs_recv_p, rs_recv_m,
    total, y_send, y_recv, new_w, acc, row_m, row_l, first_out, rows,
    power, wanted, asked, choose, terms, send_rows,
    load_sem, win_send, win_recv, relay_send, relay_recv, fwd_send, mid_recv,
    rsp_send, rsp_recv, rsm_send, rsm_recv, ys_send, ys_recv,
    agp_send, agp_recv, agm_send, agm_recv,
    pow_send, pow_recv, idx_send, idx_recv, a2a_send, a2a_recv, own_sem,
):
    T, D = q.shape
    F = w.shape[1]
    FR = F // Z
    N = Y * Z
    SEG = T // N
    CR = T // CHUNKS
    s = lax.axis_index("seq")
    h = lax.axis_index("head")
    z = s // Y
    y = s % Y

    def seq_at(zz, yy):
        return lax.rem(zz + Z, Z) * Y + lax.rem(yy + Y, Y)

    up = seq_at(z + 1, y)
    down = seq_at(z - 1, y)

    def remote(src, dst, ssem, rsem, seq):
        return pltpu.make_async_remote_copy(
            src_ref=src, dst_ref=dst, send_sem=ssem, recv_sem=rsem,
            device_id={"seq": seq}, device_id_type=MESH,
        )

    loads = [
        pltpu.make_async_copy(k_hbm, kv.at[0, 0], load_sem.at[0]),
        pltpu.make_async_copy(v_hbm, kv.at[0, 1], load_sem.at[1]),
        pltpu.make_async_copy(w_hbm, w, load_sem.at[2]),
        pltpu.make_async_copy(q_hbm, q, load_sem.at[3]),
    ]
    for copy in loads:
        copy.start()

    barrier = pltpu.get_barrier_semaphore()
    near = [up, down] + [seq_at(z, y + k) for k in range(1, Y)]
    for partner in near:
        pl.semaphore_signal(barrier, inc=1, device_id={"seq": partner}, device_id_type=MESH)
    for k in range(1, H):
        pl.semaphore_signal(
            barrier, inc=1, device_id={"head": lax.rem(h + k, H)}, device_id_type=MESH
        )
    for g in range(128 // SEG):
        line = slot_ref[...] if g == 0 else pltpu.roll(slot_ref[...], 128 - SEG * g, 1)
        for i in range(T // 128):
            e = i * (128 // SEG) + g
            wanted[e] = line[i : i + 1, :] - e * T
    pl.semaphore_wait(barrier, len(near) + H - 1)
    loads[0].wait()
    loads[1].wait()

    def rows_of(i):
        return pl.ds(i * CR, CR)

    def zhop(i):
        return remote(
            kv.at[0, :, rows_of(i)], kv.at[Y, :, rows_of(i)],
            win_send.at[Y, i], win_recv.at[Y, i], up,
        )

    def spread(k, i):
        src = jnp.where(y + k < Y, 0, Y)
        return remote(
            kv.at[src, :, rows_of(i)], kv.at[k, :, rows_of(i)],
            win_send.at[k, i], win_recv.at[k, i], seq_at(z, y + k),
        )

    def over(j, i):
        src = jnp.where(y + 2 < Y, 0, Y)
        return remote(
            kv.at[src, j, rows_of(i)], relay.at[j, rows_of(i)],
            relay_send.at[j, i], relay_recv.at[j, i], seq_at(z, y + (1 if j == 0 else -1)),
        )

    def forward(j, i):
        return remote(
            relay.at[j, rows_of(i)], kv.at[2, j, rows_of(i)],
            fwd_send.at[j, i], mid_recv.at[j, i], seq_at(z, y + (1 if j == 0 else -1)),
        )

    AHEAD = 3
    for i in range(AHEAD):
        zhop(i).start()

    def window_step(i):
        if i < CHUNKS:
            if i + AHEAD < CHUNKS:
                zhop(i + AHEAD).start()
            zhop(i).wait_recv()
            for j in range(2):
                over(j, i).start()
            spread(1, i).start()
            spread(3, i).start()
        if 1 <= i <= CHUNKS:
            for j in range(2):
                over(j, i - 1).wait_recv()
                forward(j, i - 1).start()

    first_len = len_ref[0]
    lane_member = (s * T + lax.broadcasted_iota(jnp.int32, (1, T), 1)) < first_len
    loads[2].wait()
    def chunk_of(zz):
        return lax.rem(zz + 2 * Z, Z)

    HR = FR // SUB
    units = [(c, b) for c in (2, 1, 0) for b in range(SUB)]

    def at_rows(u):
        return pl.ds(u[1] * HR, HR)

    def slot(u):
        return u[0] * SUB + u[1]

    def piece(u, zz):
        first = pl.multiple_of(chunk_of(zz) * FR + u[1] * HR, HR)
        return grad[u[0], pl.ds(first, HR), :]

    def rs_up(t, u):
        return remote(
            rs_send_p.at[t, u[0], at_rows(u)], rs_recv_p.at[t, u[0], at_rows(u)],
            rsp_send.at[t, slot(u)], rsp_recv.at[t, slot(u)], up,
        )

    def rs_down(t, u):
        return remote(
            rs_send_m.at[t, u[0], at_rows(u)], rs_recv_m.at[t, u[0], at_rows(u)],
            rsm_send.at[t, slot(u)], rsm_recv.at[t, slot(u)], down,
        )

    def rs_step(t, u):
        if t < DOWN:
            value = piece(u, z - DOWN + t)
            if t > 0:
                rs_down(t - 1, u).wait_recv()
                value = value + rs_recv_m[t - 1, u[0], at_rows(u)].astype(f32)
            rs_send_m[t, u[0], at_rows(u)] = value.astype(bf16)
            rs_down(t, u).start()
        if t < UP:
            value = piece(u, z + UP - t)
            if t > 0:
                rs_up(t - 1, u).wait_recv()
                value = value + rs_recv_p[t - 1, u[0], at_rows(u)].astype(f32)
            rs_send_p[t, u[0], at_rows(u)] = value.astype(bf16)
            rs_up(t, u).start()

    early = list(range(Z // 4, Z // 4 + Z // 2))
    late = list(range(-(Z // 4), Z // 2 - Z // 4))

    def hidden_terms(offsets):
        gate_w, up_w, down_w = (
            jnp.concatenate(
                [w[c, pl.ds(pl.multiple_of(chunk_of(z + o) * FR, FR), FR), :] for o in offsets],
                axis=0,
            )
            for c in range(3)
        )
        gate_pre = dot_t(gate_w, kv[0, 0])
        up_pre = dot_t(up_w, kv[0, 0])
        sig_gate = jax.nn.sigmoid(gate_pre)
        gated = gate_pre * sig_gate
        terms[2] = jnp.where(lane_member, gated * up_pre, 0.0).astype(bf16)
        back = jnp.where(lane_member, dot_t(down_w, kv[0, 1]), 0.0)
        terms[1] = (back * gated).astype(bf16)
        terms[0] = (back * up_pre * sig_gate * (1.0 + gate_pre * (1.0 - sig_gate))).astype(bf16)

    def weight_terms(offsets, c):
        value = dot_n(terms[c], kv[0, 1 if c == 2 else 0])
        for i, o in enumerate(offsets):
            first = pl.multiple_of(chunk_of(z + o) * FR, FR)
            grad[c, pl.ds(first, FR), :] = value[i * FR : (i + 1) * FR, :]

    hidden_terms(early)
    for c in (2, 1, 0):
        weight_terms(early, c)
        for b in range(SUB):
            rs_step(0, (c, b))
    window_step(0)
    window_step(1)
    loads[3].wait()

    exponent = math.log2(math.e) / math.sqrt(D)
    HALF = T // 2

    def attend(d, kh, qh):
        span = pl.ds(qh * HALF, HALF)
        part = pl.ds(kh * HALF, HALF)
        scores = dot_t(q[span, :], kv[d, 0, part, :])
        if d in (0, Y):
            behind = (
                lax.broadcasted_iota(jnp.int32, (HALF, HALF), 0)
                - lax.broadcasted_iota(jnp.int32, (HALF, HALF), 1)
                + ((qh - kh) * HALF + d * T)
            )
            scores = jnp.where((behind >= 0) & (behind < WIN), scores, -jnp.inf)
        if d > 0:
            scores = scores + jnp.where(s >= d, 0.0, -jnp.inf)
        peak = jnp.max(scores, axis=1, keepdims=True)
        if d == 0 and kh == 0:
            expo = jnp.exp2((scores - peak) * exponent)
            row_l[span, :] = jnp.broadcast_to(jnp.sum(expo, axis=1, keepdims=True), (HALF, 128))
            acc[span, :] = dot_n(expo.astype(bf16), kv[d, 1, part, :])
        else:
            before = row_m[span, :][:, 0:1]
            peak = jnp.maximum(before, peak)
            decay = jnp.exp2((before - peak) * exponent)
            expo = jnp.exp2((scores - peak) * exponent)
            row_l[span, :] = row_l[span, :] * decay + jnp.sum(expo, axis=1, keepdims=True)
            acc[span, :] = acc[span, :] * decay + dot_n(expo.astype(bf16), kv[d, 1, part, :])
        row_m[span, :] = jnp.broadcast_to(peak, (HALF, 128))

    def swiglu(inputs, gate_w, up_w, down_w):
        gate = dot_t(inputs, gate_w)
        hidden = (gate * jax.nn.sigmoid(gate) * dot_t(inputs, up_w)).astype(bf16)
        return dot_n(hidden, down_w).astype(bf16)

    def early_fast(part):
        span = pl.ds(part * (T // 4), T // 4)
        first_out[span, :] = swiglu(q[span, :], w[0], w[1], w[2])

    fillers = [functools.partial(attend, 0, 0, qh) for qh in range(2)]
    fillers += [functools.partial(attend, 0, 1, 1)]
    fillers += [functools.partial(early_fast, part) for part in range(4)]
    steps = max(UP, DOWN)
    seen = 2
    for t in range(1, steps):
        for u in units:
            rs_step(t, u)
        window_step(seen)
        seen += 1
        if t == 1:
            hidden_terms(late)
        elif t == 2:
            for c in (2, 1, 0):
                weight_terms(late, c)
        elif fillers:
            fillers.pop(0)()
    if steps < 3:
        for c in (2, 1, 0):
            weight_terms(late, c)

    def y_copy(k, c):
        return remote(
            y_send.at[c], y_recv.at[k - 1, c], ys_send.at[k - 1, c], ys_recv.at[k - 1, c],
            seq_at(z, y + k),
        )

    for c in (2, 1, 0):
        for b in range(SUB):
            u = (c, b)
            value = piece(u, z)
            rs_down(DOWN - 1, u).wait_recv()
            value = value + rs_recv_m[DOWN - 1, c, at_rows(u)].astype(f32)
            rs_up(UP - 1, u).wait_recv()
            total[c, at_rows(u)] = value + rs_recv_p[UP - 1, c, at_rows(u)].astype(f32)
        value = total[c]
        y_send[c] = value.astype(bf16)
        for k in range(1, Y):
            y_copy(k, c).start()
    while fillers:
        fillers.pop(0)()

    def idx_body(k, carry):
        target = lax.rem(s + k, N)
        remote(wanted.at[target], asked.at[s], idx_send, idx_recv, target).start()
        return carry

    group_count = jnp.full((1, D), first_len, jnp.int32).astype(f32)
    rate = lr_ref[0] / group_count
    for c in (2, 1, 0):
        value = total[c]
        for k in range(1, Y):
            y_copy(k, c).wait_recv()
            value = value + y_recv[k - 1, c].astype(f32)
        previous = w[c, pl.ds(pl.multiple_of(z * FR, FR), FR), :].astype(f32)
        updated = previous + rate * value
        old_norm = jnp.sqrt(jnp.sum(previous * previous, axis=1, keepdims=True) + eps)
        new_norm = jnp.sqrt(jnp.sum(updated * updated, axis=1, keepdims=True) + eps)
        new_w[z, c] = (updated * (old_norm / new_norm)).astype(bf16)

    def ag_copy(at, t, u, ssem, rsem, seq):
        part = new_w.at[at, u[0], at_rows(u)]
        return remote(part, part, ssem.at[t, slot(u)], rsem.at[t, slot(u)], seq)

    def ag_up(t, u):
        return ag_copy(chunk_of(z - t), t, u, agp_send, agp_recv, up)

    def ag_down(t, u):
        return ag_copy(chunk_of(z + t), t, u, agm_send, agm_recv, down)

    def ag_wait_up(t, u):
        ag_copy(chunk_of(z - 1 - t), t, u, agp_send, agp_recv, up).wait_recv()

    def ag_wait_down(t, u):
        ag_copy(chunk_of(z + 1 + t), t, u, agm_send, agm_recv, down).wait_recv()

    def block_ready(d, kh):
        for i in range(kh * CHUNKS // 2, (kh + 1) * CHUNKS // 2):
            if d == 2:
                for j in range(2):
                    forward(j, i).wait_recv()
            elif d != Y:
                spread(d, i).wait_recv()

    def block(d, kh, qh):
        if qh == 0:
            block_ready(d, kh)
        attend(d, kh, qh)

    fillers = [
        functools.partial(block, d, kh, qh)
        for kh in range(2) for d in (Y, 1, 3, 2) for qh in range(2)
        if (d, kh, qh) != (Y, 0, 1)
    ]
    def find_rows():
        pltpu.make_async_copy(
            asked.at[pl.ds(0, N - 1)], asked.at[pl.ds(0, N - 1)], idx_recv
        ).wait()
        lines = jnp.broadcast_to(asked[...].astype(f32), (N, SEG, 128)).reshape(T, 128)
        lane = lax.broadcasted_iota(jnp.int32, (T, 128), 1)
        spot = lax.rem(lax.broadcasted_iota(jnp.int32, (T, 128), 0), SEG)
        picked = jnp.sum(jnp.where(lane == spot, lines, 0.0), axis=1, keepdims=True)
        column = lax.broadcasted_iota(jnp.int32, (T, T), 1).astype(f32)
        choose[...] = jnp.where(column == picked, 1.0, 0.0).astype(bf16)

    near_set = list(range(-((Z // 2) // 2), (Z // 2) - (Z // 2) // 2))
    far_set = [o for o in range(-UP, DOWN + 1) if o not in near_set]

    def partial_fast(offsets):
        gate_w, up_w, down_w = (
            jnp.concatenate([new_w[chunk_of(z + o), c] for o in offsets], axis=0) for c in range(3)
        )
        gate = dot_t(q[...], gate_w)
        hidden = (gate * jax.nn.sigmoid(gate) * dot_t(q[...], up_w)).astype(bf16)
        return dot_n(hidden, down_w)

    def near_fast():
        rows[...] = partial_fast(near_set)

    extra = [find_rows]
    for t in range(steps):
        for u in units:
            if t < DOWN:
                if t > 0:
                    ag_wait_down(t - 1, u)
                ag_down(t, u).start()
            if t < UP:
                if t > 0:
                    ag_wait_up(t - 1, u)
                ag_up(t, u).start()
        if t == 0:
            lax.fori_loop(1, N, idx_body, 0)
            asked[s] = wanted[s]
        for _ in range(1):
            if seen <= CHUNKS:
                window_step(seen)
                seen += 1
        for _ in range(2):
            if fillers and seen > (CHUNKS if len(fillers) <= 8 else CHUNKS // 2):
                fillers.pop(0)()
        if t == steps - 3:
            find_rows()
            extra.clear()
    while seen <= CHUNKS:
        window_step(seen)
        seen += 1
    while fillers:
        fillers.pop(0)()
    for step in extra:
        step()
    if steps <= 2:
        for u in units:
            ag_wait_down(DOWN - 1, u)
            ag_wait_up(UP - 1, u)
    near_fast()
    attention = (acc[...] / row_l[...][:, 0:1]).astype(bf16)
    acc[...] = dot_n(choose[...], attention)
    if steps > 2:
        for u in units:
            ag_wait_down(DOWN - 1, u)
            ag_wait_up(UP - 1, u)

    second = (rows[...] + partial_fast(far_set)).astype(bf16)
    member = (s * T + lax.broadcasted_iota(jnp.int32, (T, D), 0)) < first_len
    fast = jnp.where(member, first_out[...].astype(f32), second.astype(f32))
    summed = attention.astype(f32) + fast
    square = summed * summed
    coarse = square.astype(bf16)
    fine = (square - coarse.astype(f32)).astype(bf16)
    ones = jnp.ones((8, D), bf16)
    power[h] = (dot_t(ones, coarse) + dot_t(ones, fine))[0:1, :]

    def pow_copy(k):
        return pltpu.make_async_remote_copy(
            src_ref=power.at[h], dst_ref=power.at[h],
            send_sem=pow_send.at[k - 1], recv_sem=pow_recv.at[k - 1],
            device_id={"head": lax.rem(h + k, H)}, device_id_type=MESH,
        )

    for k in range(1, H):
        pow_copy(k).start()
    rows[...] = acc[...] + dot_n(choose[...], fast.astype(bf16))
    for k in range(1, H):
        pow_copy(k).wait_recv()
    strength = power[0]
    for k in range(1, H):
        strength = strength + power[k]
    row_scale = lax.rsqrt(strength / (H * D) + eps)

    GROUPS = 4
    NG = N // GROUPS
    TG = T // GROUPS
    for far in (2, 1, 3, 0):
        g = lax.rem(s // NG + far, GROUPS)
        span = pl.ds(pl.multiple_of(g * TG, TG), TG)
        factor = jnp.sum(choose[span, :].astype(f32) * row_scale, axis=1, keepdims=True)
        normed = rows[span, :] * factor * gain_ref[...]
        send_rows[pl.ds(g * NG, NG)] = normed.reshape(NG, SEG, D).astype(bf16)

        def a2a_body(k, carry):
            target = g * NG + k

            @pl.when(target != s)
            def _():
                remote(send_rows.at[target], out_ref.at[s], a2a_send, a2a_recv, target).start()

            return carry

        lax.fori_loop(0, NG, a2a_body, 0)
    own = pltpu.make_async_copy(send_rows.at[s], out_ref.at[s], own_sem)
    own.start()

    for i in range(CHUNKS):
        zhop(i).wait_send()
        spread(1, i).wait_send()
        spread(3, i).wait_send()
        for j in range(2):
            over(j, i).wait_send()
            forward(j, i).wait_send()
    for u in units:
        for t in range(UP):
            rs_up(t, u).wait_send()
            ag_up(t, u).wait_send()
        for t in range(DOWN):
            rs_down(t, u).wait_send()
            ag_down(t, u).wait_send()
    for c in range(3):
        for k in range(1, Y):
            y_copy(k, c).wait_send()
    for k in range(1, H):
        pow_copy(k).wait_send()
    pltpu.make_async_copy(wanted.at[pl.ds(0, N - 1)], wanted.at[pl.ds(0, N - 1)], idx_send).wait()
    own.wait()
    pltpu.make_async_copy(
        send_rows.at[pl.ds(0, N - 1)], send_rows.at[pl.ds(0, N - 1)], a2a_send
    ).wait()
    pltpu.make_async_copy(
        out_ref.at[pl.ds(0, N - 1)], out_ref.at[pl.ds(0, N - 1)], a2a_recv
    ).wait()


def solution(mesh, window=WINDOW):
    N = mesh.shape["seq"]
    H = mesh.shape["head"]

    def per_device(q, k, v, weights, learn_rate, out_gain, group_lengths, slot_order):
        T, _, D = q.shape
        F = weights.shape[0]
        Y = window // T
        Z = N // Y
        UP = min(UP_HOPS, Z // 2)
        DOWN = Z - 1 - UP
        FR = F // Z
        SEG = T // N
        dma = pltpu.SemaphoreType.DMA
        VMEM = pltpu.VMEM
        any_spec = pl.BlockSpec(memory_space=pl.ANY)
        vmem_spec = pl.BlockSpec(memory_space=pltpu.VMEM)
        smem_spec = pl.BlockSpec(memory_space=pltpu.SMEM)
        out = pl.pallas_call(
            functools.partial(layer_kernel, Y, Z, H, UP, DOWN, window),
            out_shape=jax.ShapeDtypeStruct((N, SEG, D), bf16),
            in_specs=[any_spec] * 4 + [smem_spec, vmem_spec, smem_spec, vmem_spec],
            out_specs=any_spec,
            scratch_shapes=[
                VMEM((T, D), bf16),
                VMEM((Y + 1, 2, T, D), bf16),
                VMEM((3, F, D), bf16),
                VMEM((2, T, D), bf16),
                VMEM((3, F, D), f32),
                VMEM((UP, 3, FR, D), bf16),
                VMEM((max(DOWN, 1), 3, FR, D), bf16),
                VMEM((UP, 3, FR, D), bf16),
                VMEM((max(DOWN, 1), 3, FR, D), bf16),
                VMEM((3, FR, D), f32),
                VMEM((3, FR, D), bf16),
                VMEM((Y - 1, 3, FR, D), bf16),
                VMEM((Z, 3, FR, D), bf16),
                VMEM((T, D), f32),
                VMEM((T, 128), f32),
                VMEM((T, 128), f32),
                VMEM((T, D), bf16),
                VMEM((T, D), f32),
                VMEM((H, 1, T), f32),
                VMEM((N, 1, 128), jnp.int32),
                VMEM((N, 1, 128), jnp.int32),
                VMEM((T, T), bf16),
                VMEM((3, F // 2, T), bf16),
                VMEM((N, SEG, D), bf16),
                dma((4,)),
                dma((Y + 1, CHUNKS)),
                dma((Y + 1, CHUNKS)),
                dma((2, CHUNKS)),
                dma((2, CHUNKS)),
                dma((2, CHUNKS)),
                dma((2, CHUNKS)),
                dma((UP, 3 * SUB)),
                dma((UP, 3 * SUB)),
                dma((max(DOWN, 1), 3 * SUB)),
                dma((max(DOWN, 1), 3 * SUB)),
                dma((Y - 1, 3)),
                dma((Y - 1, 3)),
                dma((UP, 3 * SUB)),
                dma((UP, 3 * SUB)),
                dma((max(DOWN, 1), 3 * SUB)),
                dma((max(DOWN, 1), 3 * SUB)),
                dma((max(H - 1, 1),)),
                dma((max(H - 1, 1),)),
                dma,
                dma,
                dma,
                dma,
                dma,
            ],
            compiler_params=pltpu.CompilerParams(
                collective_id=0, has_side_effects=True, vmem_limit_bytes=60 * 1024 * 1024
            ),
            name="ttt_layer",
        )(
            q.reshape(T, D), k.reshape(T, D), v.reshape(T, D),
            jnp.transpose(weights.reshape(F, 3, D), (1, 0, 2)),
            learn_rate, out_gain, group_lengths, slot_order.reshape(T // 128, 128),
        )
        return out.reshape(T, 1, D)

    return jax.shard_map(
        per_device,
        mesh=mesh,
        in_specs=(
            P("seq", "head", None),
            P("seq", "head", None),
            P("seq", "head", None),
            P(None, "head", None, None),
            P("head"),
            P("head", None),
            P(),
            P("seq"),
        ),
        out_specs=P("seq", "head", None),
        check_vma=False,
    )
```
